32 devices in a mesh: blade: 1, prow: 4 (over x, core), pcol: 8 (over z, y).
Axes of the slice: x: 2, y: 2, z: 4, core: 2. Of those that a mesh axis runs over, the one named last changes fastest.
Arguments:
- factor: float32 [4, 4, 512, 4, 8, 256], P('blade', 'prow', None, None, 'pcol'), may hold values from -0.03125 to 0.03125
- inverses: float32 [4, 8, 256, 4, 512], P('blade', 'pcol', None, 'prow'), as said below
- targets: float32 [8, 3, 8192], P('blade'), may hold values from -6 to 6
- anchors: float32 [3, 8192], P('blade'), may hold values from 0 to 1, as said below
- nodes: float32 [3, 16, 128, 128], P('blade', 'prow', 'pcol'), as said below
Outputs:
- coefficients: float32 [8, 3, 8192], P('blade')
- moved: float32 [8, 3, 16, 128, 128], P('blade', None, 'prow', 'pcol')
- jacobian: float32 [8, 16, 128, 128], P('blade', 'prow', 'pcol')
The draws below stay inside these ranges and needn't reach their ends.
Inputs may be any that keep to these rules, and one draw needn't show every extreme that they name: `inverses`: 4 blocks of 2048 x 2048 real entries. `anchors`: positions in the unit cube. `nodes`: positions inside a box around the unit cube, ordered along span, chord and normal.
All inputs are finite; a program needn't handle non-finite values.
Results may differ from the reference program's by a relative error of at most 0.0003.
Values sent between devices are 32-bit elements; how exact they have to be, the bound alone decides.
A program may use at most 64 MiB of HBM per device.

```python
import math
import jax
import jax.numpy as jnp
from jax import lax

POINTS = 8192
NB = 2048
KB = 4
NBR = 512
NBC = 256
NT = 8
NN = 128
NS = 16
NC = 128
N_PROW = 4
N_PCOL = 8


def draw_inverses(key, part):
    shape = (KB, N_PCOL, NBC, N_PROW, NBR)
    row_pos = lax.broadcasted_iota(jnp.int32, shape, 1) * NBC + lax.broadcasted_iota(jnp.int32, shape, 2)
    col_pos = lax.broadcasted_iota(jnp.int32, shape, 3) * NBR + lax.broadcasted_iota(jnp.int32, shape, 4)
    identity = (row_pos == col_pos).astype(jnp.float32)
    noise = jnp.clip(jax.random.normal(key, shape, jnp.float32), -4.0, 4.0)
    return identity + 0.4 / math.sqrt(NB) * noise


def draw_anchors(key, part):
    unit = jax.random.uniform(key, (3, POINTS), jnp.float32, 0.0, 1.0)
    normal_pos = 0.6 * unit[2] * unit[2]
    return jnp.stack([unit[0], unit[1], normal_pos], axis=0)


def draw_nodes(key, part):
    shape = (NS, NC, NN)
    span_pos = (lax.broadcasted_iota(jnp.float32, shape, 0) + 0.5) / NS
    chord_pos = (lax.broadcasted_iota(jnp.float32, shape, 1) + 0.5) / NC
    normal_pos = (lax.broadcasted_iota(jnp.float32, shape, 2) + 0.5) / NN
    noise = 0.15 * jnp.clip(jax.random.normal(key, (3,) + shape, jnp.float32), -4.0, 4.0)
    span_pos = span_pos + noise[0] / NS
    chord_pos = chord_pos + noise[1] / NC
    normal_pos = normal_pos + noise[2] / NN
    return jnp.stack([span_pos, chord_pos, normal_pos], axis=0)


def steps_of(stream_key, shape, shards, low, largest):
    loudness = 1.0
    for position, blocks in shards:
        draws = jax.random.uniform(jax.random.fold_in(jax.random.fold_in(stream_key, 6), position), (blocks,), jnp.float32, low / len(shards), largest / len(shards))
        loudness = loudness * jnp.repeat(jnp.exp(draws), shape[position] // blocks).reshape((-1,) + (1,) * (len(shape) - 1 - position))
    return loudness


def gaussian(stream_key, shape, width, limit, split=(), dtype=jnp.bfloat16):
    result = jax.random.normal(stream_key, shape, jnp.float32) * width
    if len(split) > 0:
        result = steps_of(stream_key, shape, split, -0.22, 0.18) * result
    return jnp.clip(result, min=-limit, max=limit).astype(dtype)


def setup_inputs(seed: int = 0, part: int = 0) -> dict:
    key_of = jax.random.split(jax.random.key(seed), 6)
    part_keys = jax.random.split(jax.random.fold_in(key_of[5], part), 6)
    return {
        "factor": gaussian(part_keys[0], (KB, N_PROW, NBR, KB, N_PCOL, NBC), (4 * POINTS) ** -0.5, 0.03125, ((1, 4), (4, 8)), jnp.float32),
        "inverses": draw_inverses(jax.random.fold_in(jax.random.fold_in(key_of[5], part), 71), part),
        "targets": gaussian(part_keys[2], (NT, 3, POINTS), 1.0, 6.0, (), jnp.float32),
        "anchors": draw_anchors(jax.random.fold_in(jax.random.fold_in(key_of[5], part), 71), part),
        "nodes": draw_nodes(jax.random.fold_in(jax.random.fold_in(key_of[5], part), 71), part),
    }


support_radius = 0.1
highest = lax.Precision.HIGHEST

def wendland(dist_sq):
    scaled_dist = jnp.sqrt(dist_sq) / support_radius
    falloff = jnp.maximum(1.0 - scaled_dist, 0.0)
    return falloff ** 4 * (4.0 * scaled_dist + 1.0)

def extend(values, axis_pos):
    extent = values.shape[axis_pos]
    low_layer = 2.0 * lax.slice_in_dim(values, 0, 1, axis=axis_pos) - lax.slice_in_dim(values, 1, 2, axis=axis_pos)
    high_layer = 2.0 * lax.slice_in_dim(values, extent - 1, extent, axis=axis_pos) - lax.slice_in_dim(values, extent - 2, extent - 1, axis=axis_pos)
    return jnp.concatenate([low_layer, values, high_layer], axis=axis_pos)

def jacobian_of(extended, scales):
    d_span = (extended[:, :, 2:, 1:-1, 1:-1] - extended[:, :, :-2, 1:-1, 1:-1]) * scales[0]
    d_chord = (extended[:, :, 1:-1, 2:, 1:-1] - extended[:, :, 1:-1, :-2, 1:-1]) * scales[1]
    d_normal = (extended[:, :, 1:-1, 1:-1, 2:] - extended[:, :, 1:-1, 1:-1, :-2]) * scales[2]
    cross_first = d_chord[:, 1] * d_normal[:, 2] - d_chord[:, 2] * d_normal[:, 1]
    cross_second = d_chord[:, 2] * d_normal[:, 0] - d_chord[:, 0] * d_normal[:, 2]
    cross_third = d_chord[:, 0] * d_normal[:, 1] - d_chord[:, 1] * d_normal[:, 0]
    return d_span[:, 0] * cross_first + d_span[:, 1] * cross_second + d_span[:, 2] * cross_third

def reference(factor, inverses, targets, anchors, nodes):
    row_count = 3 * NT
    blocks = factor.reshape(KB, NB, KB, NB).transpose(0, 2, 1, 3)
    block_inverses = inverses.reshape(KB, NB, NB)
    right_sides = targets.reshape(row_count, KB, NB)
    forward = jnp.zeros((row_count, KB, NB), jnp.float32)
    for block_id in range(KB):
        partial_value = jnp.einsum('jab,wjb->wa', blocks[block_id], forward, precision=highest)
        solved = jnp.einsum('ab,wb->wa', block_inverses[block_id], right_sides[:, block_id] - partial_value, precision=highest)
        forward = forward.at[:, block_id].set(solved)
    coeffs = jnp.zeros((row_count, KB, NB), jnp.float32)
    for block_id in reversed(range(KB)):
        partial_value = jnp.einsum('jab,wja->wb', blocks[:, block_id], coeffs, precision=highest)
        solved = jnp.einsum('ba,wb->wa', block_inverses[block_id], forward[:, block_id] - partial_value, precision=highest)
        coeffs = coeffs.at[:, block_id].set(solved)
    coef_matrix = coeffs.reshape(row_count, POINTS)
    flat = nodes.reshape(3, -1)
    node_count = flat.shape[1]
    block_size = math.gcd(node_count, 1024)
    node_groups = flat.reshape(3, node_count // block_size, block_size).transpose(1, 0, 2)

    def deform(node_group):
        dist_sq = (node_group[0][:, None] - anchors[0][None, :]) ** 2
        dist_sq = dist_sq + (node_group[1][:, None] - anchors[1][None, :]) ** 2
        dist_sq = dist_sq + (node_group[2][:, None] - anchors[2][None, :]) ** 2
        return lax.dot_general(coef_matrix, wendland(dist_sq), (((1,), (1,)), ((), ())), precision=highest)
    shifts = lax.map(deform, node_groups)
    shifts = shifts.transpose(1, 0, 2).reshape(NT, 3, NS, NC, NN)
    moved = nodes[None] + 2.0 / math.sqrt(POINTS) * shifts
    extended = extend(extend(extend(moved, 2), 3), 4)
    jacobian = jacobian_of(extended, (NS / 2.0, NC / 2.0, NN / 2.0))
    return (coeffs.reshape(NT, 3, POINTS), moved, jacobian)
```

```python
import functools
import math

import jax
import jax.numpy as jnp
from jax import lax
from jax.experimental import pallas as pl
from jax.experimental.pallas import tpu as pltpu
from jax.sharding import PartitionSpec as P

support_radius = 0.1
reach = support_radius + 1e-4
BLOCK = 128
CHUNK = 256
highest = lax.Precision.HIGHEST


def deform_kernel(order_ref, bounds_ref, stacked_ref, nodes_ref, out_ref, table, gathered, coefs, sums):
    rows = sums.shape[0]
    groups = nodes_ref.shape[0]
    width = nodes_ref.shape[2]
    blocks = table.shape[0] // BLOCK

    @pl.loop(0, blocks)
    def _(b):
        start = pl.multiple_of(b * BLOCK, BLOCK)
        piece = stacked_ref[:, pl.ds(start, BLOCK)]
        padding = jnp.zeros((BLOCK - piece.shape[0], BLOCK), jnp.float32)
        table[pl.ds(start, BLOCK), :] = jnp.concatenate([piece, padding], axis=0).T

    @pl.loop(bounds_ref[2 * groups], bounds_ref[2 * groups + 1])
    def _(b):
        start = pl.multiple_of(b * BLOCK, BLOCK)

        @pl.loop(0, BLOCK // 16)
        def _(i):
            base = start + i * 16
            for j in range(16):
                gathered[pl.ds(base + j, 1), :] = table[pl.ds(order_ref[base + j], 1), :]

        turned = gathered[pl.ds(start, BLOCK), :].T
        exact = turned[:rows]
        high = exact.astype(jnp.bfloat16)
        low = (exact - high.astype(jnp.float32)).astype(jnp.bfloat16)
        coefs[b, 0] = jnp.concatenate([high, low], axis=0)

    for g in range(groups):
        sums[...] = jnp.zeros_like(sums)

        @pl.loop(bounds_ref[2 * g], bounds_ref[2 * g + 1])
        def _(b):
            start = pl.multiple_of(b * BLOCK, BLOCK)
            places = gathered[pl.ds(start, BLOCK), :]
            px = jnp.broadcast_to(places[:, rows : rows + 1], (BLOCK, CHUNK))
            py = jnp.broadcast_to(places[:, rows + 1 : rows + 2], (BLOCK, CHUNK))
            pz = jnp.broadcast_to(places[:, rows + 2 : rows + 3], (BLOCK, CHUNK))
            both = coefs[b, 0]
            for c in range(width // CHUNK):
                cut = slice(c * CHUNK, (c + 1) * CHUNK)
                dx = nodes_ref[g, 0:1, cut] - px
                dy = nodes_ref[g, 1:2, cut] - py
                dz = nodes_ref[g, 2:3, cut] - pz
                dist_sq = dx * dx + dy * dy + dz * dz
                dist = dist_sq * lax.rsqrt(jnp.maximum(dist_sq, 1e-30))
                falloff = jnp.maximum(1.0 - dist * (1.0 / support_radius), 0.0)
                square = falloff * falloff
                phi = square * square * (5.0 - 4.0 * falloff)
                phi_high = phi.astype(jnp.bfloat16)
                phi_low = (phi - phi_high.astype(jnp.float32)).astype(jnp.bfloat16)
                first = jnp.dot(both, phi_high, preferred_element_type=jnp.float32)
                second = jnp.dot(both, phi_low, preferred_element_type=jnp.float32)
                sums[:, cut] += first[:rows] + first[rows:] + second[:rows]

        out_ref[g] = sums[...]


def deform(coef_matrix, anchors, nodes):
    rows, points = coef_matrix.shape
    spans = nodes.shape[1]
    width = nodes.shape[2] * nodes.shape[3]
    low = jnp.min(nodes, axis=(2, 3)) - reach
    high = jnp.max(nodes, axis=(2, 3)) + reach
    box_low = jnp.min(low, axis=1)[:, None]
    box_high = jnp.max(high, axis=1)[:, None]
    near = jnp.all((anchors >= box_low) & (anchors <= box_high), axis=0)
    keys = jnp.where(near, anchors[0], 3e38)
    _, order = lax.sort((keys, lax.iota(jnp.int32, points)), num_keys=1, is_stable=False)
    firsts = jnp.sum(keys[None, :] < low[0][:, None], axis=1, dtype=jnp.int32) // BLOCK
    lasts = jnp.sum(keys[None, :] <= high[0][:, None], axis=1, dtype=jnp.int32)
    lasts = (lasts + BLOCK - 1) // BLOCK
    bounds = jnp.stack([firsts, lasts], axis=1).reshape(-1)
    bounds = jnp.concatenate([bounds, jnp.min(firsts)[None], jnp.max(lasts)[None]])
    stacked = jnp.concatenate([coef_matrix, anchors, jnp.zeros((5, points), jnp.float32)], axis=0)
    grouped = nodes.reshape(3, spans, width).transpose(1, 0, 2)
    smem = pl.BlockSpec(memory_space=pltpu.SMEM)
    vmem = pl.BlockSpec(memory_space=pltpu.VMEM)
    shifts = pl.pallas_call(
        deform_kernel,
        out_shape=jax.ShapeDtypeStruct((spans, rows, width), jnp.float32),
        in_specs=[smem, smem, vmem, vmem],
        out_specs=vmem,
        scratch_shapes=[
            pltpu.VMEM((points, BLOCK), jnp.float32),
            pltpu.VMEM((points, BLOCK), jnp.float32),
            pltpu.VMEM((points // BLOCK, 1, 2 * rows, BLOCK), jnp.bfloat16),
            pltpu.VMEM((rows, width), jnp.float32),
        ],
        compiler_params=pltpu.CompilerParams(vmem_limit_bytes=40 << 20),
        name="deform",
    )(order, bounds, stacked, grouped)
    return shifts.transpose(1, 0, 2)


def jacobian_kernel(scales, edges_ref, moved_ref, below_ref, above_ref, left_ref, right_ref, out_ref):
    cells = moved_ref[0]
    spans, chords, normals = cells.shape[1:]
    at_low, at_high, at_left, at_right = [edges_ref[i] == 1 for i in range(4)]
    below = jnp.where(at_low, 2.0 * cells[:, 0] - cells[:, 1], below_ref[0])
    above = jnp.where(at_high, 2.0 * cells[:, spans - 1] - cells[:, spans - 2], above_ref[0])
    chord_pos = lax.broadcasted_iota(jnp.int32, (3, chords, normals), 1)
    normal_pos = lax.broadcasted_iota(jnp.int32, (3, chords, normals), 2)
    for s in range(spans):
        here = cells[:, s]
        before = below if s == 0 else cells[:, s - 1]
        after = above if s == spans - 1 else cells[:, s + 1]
        d_span = (after - before) * scales[0]
        left = jnp.where(at_left, 2.0 * here[:, 0:1] - here[:, 1:2], left_ref[0, :, s : s + 1])
        right = jnp.where(
            at_right,
            2.0 * here[:, chords - 1 :] - here[:, chords - 2 : chords - 1],
            right_ref[0, :, s : s + 1],
        )
        prior = jnp.where(chord_pos == 0, left, pltpu.roll(here, 1, 1))
        later = jnp.where(chord_pos == chords - 1, right, pltpu.roll(here, chords - 1, 1))
        d_chord = (later - prior) * scales[1]
        up = pltpu.roll(here, normals - 1, 2)
        down = pltpu.roll(here, 1, 2)
        inner = jnp.where(normal_pos == 0, 2.0 * here - up, down)
        outer = jnp.where(normal_pos == normals - 1, 2.0 * here - down, up)
        d_normal = (outer - inner) * scales[2]
        out_ref[0, s] = (
            d_span[0] * (d_chord[1] * d_normal[2] - d_chord[2] * d_normal[1])
            + d_span[1] * (d_chord[2] * d_normal[0] - d_chord[0] * d_normal[2])
            + d_span[2] * (d_chord[0] * d_normal[1] - d_chord[1] * d_normal[0])
        )


def shifted(edge, axis, step):
    count = lax.axis_size(axis)
    pairs = [(i, i + step) for i in range(count) if 0 <= i + step < count]
    return lax.ppermute(edge, axis, pairs)


def jacobian_of(moved):
    instances, _, spans, chords, normals = moved.shape
    row_devs, col_devs = lax.axis_size("prow"), lax.axis_size("pcol")
    prow_id, pcol_id = lax.axis_index("prow"), lax.axis_index("pcol")
    below = shifted(moved[:, :, spans - 1], "prow", 1)
    above = shifted(moved[:, :, 0], "prow", -1)
    left = shifted(moved[:, :, :, chords - 1], "pcol", 1)
    right = shifted(moved[:, :, :, 0], "pcol", -1)
    edges = jnp.stack(
        [prow_id == 0, prow_id == row_devs - 1, pcol_id == 0, pcol_id == col_devs - 1]
    ).astype(jnp.int32)
    scales = (spans * row_devs / 2.0, chords * col_devs / 2.0, normals / 2.0)

    def spec(*shape):
        return pl.BlockSpec((1,) + shape, lambda t: (t,) + (0,) * len(shape))

    return pl.pallas_call(
        functools.partial(jacobian_kernel, scales),
        grid=(instances,),
        out_shape=jax.ShapeDtypeStruct((instances, spans, chords, normals), jnp.float32),
        in_specs=[
            pl.BlockSpec(memory_space=pltpu.SMEM),
            spec(3, spans, chords, normals),
            spec(3, chords, normals),
            spec(3, chords, normals),
            spec(3, spans, normals),
            spec(3, spans, normals),
        ],
        out_specs=spec(spans, chords, normals),
        name="jacobian",
    )(edges, moved, below, above, left, right)


def halves(values):
    high = values.astype(jnp.bfloat16)
    return high, (values - high.astype(jnp.float32)).astype(jnp.bfloat16)


def product(values, high, low, dim):
    rows = values.shape[0]
    first, second = halves(values)
    dims = (((1,), (dim,)), ((), ()))
    both = lax.dot_general(
        jnp.concatenate([first, second], axis=0), high, dims, preferred_element_type=jnp.float32
    )
    rest = lax.dot_general(first, low, dims, preferred_element_type=jnp.float32)
    return both[:rows] + both[rows:] + rest


def solve_kernel(
    row_devs, col_devs, block_total, lower_ref, inverse_ref, right_ref, out_ref,
    lower_high, lower_low, inverse_high, inverse_low, forward, solved,
    parts, landed, joined, traded,
    part_send, part_recv, join_send, join_recv, trade_send, trade_recv, out_send, out_recv,
):
    prow_id = lax.axis_index("prow")
    pcol_id = lax.axis_index("pcol")
    pieces = parts.shape[1]
    base = (pcol_id // pieces) * pieces
    piece_id = lax.rem(pcol_id, pieces)
    mesh_ids = pl.DeviceIdType.MESH

    barrier = pltpu.get_barrier_semaphore()
    for o in range(1, col_devs):
        pl.semaphore_signal(
            barrier, 1, device_id={"pcol": lax.rem(pcol_id + o, col_devs)}, device_id_type=mesh_ids
        )
    for o in range(1, row_devs):
        pl.semaphore_signal(
            barrier, 1, device_id={"prow": lax.rem(prow_id + o, row_devs)}, device_id_type=mesh_ids
        )
    for p in range(lower_ref.shape[0]):
        lower_high[p], lower_low[p] = halves(lower_ref[p])
    for k in range(block_total):
        inverse_high[k], inverse_low[k] = halves(inverse_ref[k])
    pl.semaphore_wait(barrier, col_devs + row_devs - 2)

    def pair(i, j):
        return i * (i - 1) // 2 + j

    def sum_pcol(turn, values):
        for q in range(pieces):
            parts[turn, q] = values[:, q * 128 : (q + 1) * 128]
        copies = []
        for o in range(1, col_devs):
            other = lax.rem(pcol_id + o, col_devs)
            copy = pltpu.make_async_remote_copy(
                src_ref=parts.at[turn, lax.rem(other, pieces)],
                dst_ref=landed.at[turn, pcol_id],
                send_sem=part_send.at[o - 1],
                recv_sem=part_recv.at[turn, o - 1],
                device_id={"pcol": other},
                device_id_type=mesh_ids,
            )
            copy.start()
            copies.append(copy)
        landed[turn, pcol_id] = parts[turn, piece_id]
        for copy in copies:
            copy.wait()
        total = landed[turn, 0]
        for d in range(1, col_devs):
            total = total + landed[turn, d]
        joined[turn, piece_id] = total
        copies = []
        for o in range(1, pieces):
            copy = pltpu.make_async_remote_copy(
                src_ref=joined.at[turn, piece_id],
                dst_ref=joined.at[turn, piece_id],
                send_sem=join_send.at[o - 1],
                recv_sem=join_recv.at[turn, o - 1],
                device_id={"pcol": base + lax.rem(piece_id + o, pieces)},
                device_id_type=mesh_ids,
            )
            copy.start()
            copies.append(copy)
        for copy in copies:
            copy.wait()
        return jnp.concatenate([joined[turn, q] for q in range(pieces)], axis=1)

    def sum_prow(turn, values):
        traded[turn, prow_id] = values
        copies = []
        for o in range(1, row_devs):
            copy = pltpu.make_async_remote_copy(
                src_ref=traded.at[turn, prow_id],
                dst_ref=traded.at[turn, prow_id],
                send_sem=trade_send.at[o - 1],
                recv_sem=trade_recv.at[turn, o - 1],
                device_id={"prow": lax.rem(prow_id + o, row_devs)},
                device_id_type=mesh_ids,
            )
            copy.start()
            copies.append(copy)
        for copy in copies:
            copy.wait()
        total = traded[turn, 0]
        for d in range(1, row_devs):
            total = total + traded[turn, d]
        return total

    col_turn = 0
    row_turn = 0
    for k in range(block_total):
        residual = right_ref[k]
        if k > 0:
            partial = None
            for j in range(k):
                term = product(forward[j], lower_high[pair(k, j)], lower_low[pair(k, j)], 1)
                partial = term if partial is None else partial + term
            residual = residual - sum_pcol(col_turn, partial)
            col_turn += 1
        term = product(residual, inverse_high[k], inverse_low[k], 1)
        forward[k] = sum_prow(row_turn, term)
        row_turn += 1
    out_copies = []
    for k in reversed(range(block_total)):
        residual = forward[k]
        if k < block_total - 1:
            partial = None
            for j in range(k + 1, block_total):
                term = product(
                    solved[j, prow_id], lower_high[pair(j, k)], lower_low[pair(j, k)], 0
                )
                partial = term if partial is None else partial + term
            residual = residual - sum_prow(row_turn, partial)
            row_turn += 1
        term = product(residual, inverse_high[k], inverse_low[k], 0)
        solved[k, prow_id] = sum_pcol(col_turn, term)
        col_turn += 1
        for o in range(1, row_devs):
            copy = pltpu.make_async_remote_copy(
                src_ref=solved.at[k, prow_id],
                dst_ref=solved.at[k, prow_id],
                send_sem=out_send.at[k, o - 1],
                recv_sem=out_recv.at[k, o - 1],
                device_id={"prow": lax.rem(prow_id + o, row_devs)},
                device_id_type=mesh_ids,
            )
            copy.start()
            out_copies.append(copy)
    for copy in out_copies:
        copy.wait()
    width = solved.shape[3]
    for k in range(block_total):
        for d in range(row_devs):
            start = (k * row_devs + d) * width
            out_ref[:, start : start + width] = solved[k, d]


def solve(local_factor, local_inverses, right_sides):
    row_devs = lax.axis_size("prow")
    col_devs = lax.axis_size("pcol")
    block_total, row_piece, _, col_piece = local_factor.shape
    row_count = right_sides.shape[0]
    lower = jnp.stack([local_factor[i, :, j] for i in range(block_total) for j in range(i)])
    own = right_sides.reshape(row_count, block_total, row_devs, row_piece)
    own = lax.dynamic_index_in_dim(own, lax.axis_index("prow"), 2, keepdims=False)
    own = own.transpose(1, 0, 2)
    pieces = row_piece // 128
    turns = 2 * block_total - 1
    vmem = pl.BlockSpec(memory_space=pltpu.VMEM)
    dma = pltpu.SemaphoreType.DMA
    narrow = jnp.bfloat16
    wide = jnp.float32
    return pl.pallas_call(
        functools.partial(solve_kernel, row_devs, col_devs, block_total),
        out_shape=jax.ShapeDtypeStruct((row_count, block_total * row_devs * row_piece), wide),
        in_specs=[vmem, vmem, vmem],
        out_specs=vmem,
        scratch_shapes=[
            pltpu.VMEM(lower.shape, narrow),
            pltpu.VMEM(lower.shape, narrow),
            pltpu.VMEM(local_inverses.shape, narrow),
            pltpu.VMEM(local_inverses.shape, narrow),
            pltpu.VMEM((block_total, row_count, col_piece), wide),
            pltpu.VMEM((block_total, row_devs, row_count, row_piece), wide),
            pltpu.VMEM((turns, pieces, row_count, 128), wide),
            pltpu.VMEM((turns, col_devs, row_count, 128), wide),
            pltpu.VMEM((turns, pieces, row_count, 128), wide),
            pltpu.VMEM((turns, row_devs, row_count, col_piece), wide),
            dma((col_devs - 1,)),
            dma((turns, col_devs - 1)),
            dma((pieces - 1,)),
            dma((turns, pieces - 1)),
            dma((row_devs - 1,)),
            dma((turns, row_devs - 1)),
            dma((block_total, row_devs - 1)),
            dma((block_total, row_devs - 1)),
        ],
        compiler_params=pltpu.CompilerParams(
            collective_id=0, has_side_effects=True, vmem_limit_bytes=40 << 20
        ),
        name="solve",
    )(lower, local_inverses, own)


def shards(factor, inverses, targets, anchors, nodes):
    row_devs = lax.axis_size("prow")
    local_factor = factor[:, 0, :, :, 0, :]
    local_inverses = inverses[:, 0, :, 0, :]
    block_total = local_factor.shape[0]
    row_piece = local_factor.shape[1]
    block_len = row_piece * row_devs
    instances = targets.shape[0]
    row_count = instances * targets.shape[1]
    point_total = targets.shape[2]
    right_sides = targets.reshape(row_count, block_total, block_len)
    coef_matrix = solve(local_factor, local_inverses, right_sides)
    shifts = deform(coef_matrix, anchors, nodes).reshape((instances,) + nodes.shape)
    moved = nodes[None] + 2.0 / math.sqrt(point_total) * shifts
    jacobian = jacobian_of(moved)
    return (coef_matrix.reshape(instances, 3, point_total), moved, jacobian)


def solution(mesh):
    placed = (
        P("blade", "prow", None, None, "pcol", None),
        P("blade", "pcol", None, "prow", None),
        P("blade", None, None),
        P("blade", None),
        P("blade", "prow", "pcol", None),
    )
    return jax.shard_map(
        shards,
        mesh=mesh,
        in_specs=placed,
        out_specs=(
            P("blade", None, None),
            P("blade", None, "prow", "pcol", None),
            P("blade", "prow", "pcol", None),
        ),
        check_vma=False,
    )
```

```python
import functools
import math

import jax
import jax.numpy as jnp
from jax import lax
from jax.experimental import pallas as pl
from jax.experimental.pallas import tpu as pltpu
from jax.sharding import PartitionSpec as P

support_radius = 0.1
reach = support_radius + 1e-4
BLOCK = 128
CHUNK = 256
highest = lax.Precision.HIGHEST


def deform_kernel(order_ref, bounds_ref, stacked_ref, nodes_ref, out_ref, table, gathered, coefs, sums):
    rows = sums.shape[0]
    groups = nodes_ref.shape[0]
    width = nodes_ref.shape[2]
    blocks = table.shape[0] // BLOCK

    @pl.loop(0, blocks)
    def _(b):
        start = pl.multiple_of(b * BLOCK, BLOCK)
        piece = stacked_ref[:, pl.ds(start, BLOCK)]
        padding = jnp.zeros((BLOCK - piece.shape[0], BLOCK), jnp.float32)
        table[pl.ds(start, BLOCK), :] = jnp.concatenate([piece, padding], axis=0).T

    @pl.loop(bounds_ref[2 * groups], bounds_ref[2 * groups + 1])
    def _(b):
        start = pl.multiple_of(b * BLOCK, BLOCK)

        @pl.loop(0, BLOCK // 16)
        def _(i):
            base = start + i * 16
            for j in range(16):
                gathered[pl.ds(base + j, 1), :] = table[pl.ds(order_ref[base + j], 1), :]

        turned = gathered[pl.ds(start, BLOCK), :].T
        exact = turned[:rows]
        high = exact.astype(jnp.bfloat16)
        low = (exact - high.astype(jnp.float32)).astype(jnp.bfloat16)
        coefs[b, 0] = jnp.concatenate([high, low], axis=0)

    for g in range(groups):
        sums[...] = jnp.zeros_like(sums)

        @pl.loop(bounds_ref[2 * g], bounds_ref[2 * g + 1])
        def _(b):
            start = pl.multiple_of(b * BLOCK, BLOCK)
            places = gathered[pl.ds(start, BLOCK), :]
            px = jnp.broadcast_to(places[:, rows : rows + 1], (BLOCK, CHUNK))
            py = jnp.broadcast_to(places[:, rows + 1 : rows + 2], (BLOCK, CHUNK))
            pz = jnp.broadcast_to(places[:, rows + 2 : rows + 3], (BLOCK, CHUNK))
            both = coefs[b, 0]
            for c in range(width // CHUNK):
                cut = slice(c * CHUNK, (c + 1) * CHUNK)
                dx = nodes_ref[g, 0:1, cut] - px
                dy = nodes_ref[g, 1:2, cut] - py
                dz = nodes_ref[g, 2:3, cut] - pz
                dist_sq = dx * dx + dy * dy + dz * dz
                dist = dist_sq * lax.rsqrt(jnp.maximum(dist_sq, 1e-30))
                falloff = jnp.maximum(1.0 - dist * (1.0 / support_radius), 0.0)
                square = falloff * falloff
                phi = square * square * (5.0 - 4.0 * falloff)
                phi_high = phi.astype(jnp.bfloat16)
                phi_low = (phi - phi_high.astype(jnp.float32)).astype(jnp.bfloat16)
                first = jnp.dot(both, phi_high, preferred_element_type=jnp.float32)
                second = jnp.dot(both, phi_low, preferred_element_type=jnp.float32)
                sums[:, cut] += first[:rows] + first[rows:] + second[:rows]

        out_ref[g] = sums[...]


def deform(coef_matrix, anchors, nodes):
    rows, points = coef_matrix.shape
    spans = nodes.shape[1]
    width = nodes.shape[2] * nodes.shape[3]
    low = jnp.min(nodes, axis=(2, 3)) - reach
    high = jnp.max(nodes, axis=(2, 3)) + reach
    box_low = jnp.min(low, axis=1)[:, None]
    box_high = jnp.max(high, axis=1)[:, None]
    near = jnp.all((anchors >= box_low) & (anchors <= box_high), axis=0)
    keys = jnp.where(near, anchors[0], 3e38)
    _, order = lax.sort((keys, lax.iota(jnp.int32, points)), num_keys=1, is_stable=False)
    firsts = jnp.sum(keys[None, :] < low[0][:, None], axis=1, dtype=jnp.int32) // BLOCK
    lasts = jnp.sum(keys[None, :] <= high[0][:, None], axis=1, dtype=jnp.int32)
    lasts = (lasts + BLOCK - 1) // BLOCK
    bounds = jnp.stack([firsts, lasts], axis=1).reshape(-1)
    bounds = jnp.concatenate([bounds, jnp.min(firsts)[None], jnp.max(lasts)[None]])
    stacked = jnp.concatenate([coef_matrix, anchors, jnp.zeros((5, points), jnp.float32)], axis=0)
    grouped = nodes.reshape(3, spans, width).transpose(1, 0, 2)
    smem = pl.BlockSpec(memory_space=pltpu.SMEM)
    vmem = pl.BlockSpec(memory_space=pltpu.VMEM)
    shifts = pl.pallas_call(
        deform_kernel,
        out_shape=jax.ShapeDtypeStruct((spans, rows, width), jnp.float32),
        in_specs=[smem, smem, vmem, vmem],
        out_specs=vmem,
        scratch_shapes=[
            pltpu.VMEM((points, BLOCK), jnp.float32),
            pltpu.VMEM((points, BLOCK), jnp.float32),
            pltpu.VMEM((points // BLOCK, 1, 2 * rows, BLOCK), jnp.bfloat16),
            pltpu.VMEM((rows, width), jnp.float32),
        ],
        compiler_params=pltpu.CompilerParams(vmem_limit_bytes=40 << 20),
        name="deform",
    )(order, bounds, stacked, grouped)
    return shifts.transpose(1, 0, 2)


def jacobian_kernel(
    scales, row_devs, col_devs, moved_ref, out_ref,
    first, last, below, above, left, right, send, recv,
):
    instances, _, spans, chords, normals = moved_ref.shape
    prow_id = lax.axis_index("prow")
    pcol_id = lax.axis_index("pcol")
    mesh_ids = pl.DeviceIdType.MESH
    barrier = pltpu.get_barrier_semaphore()
    for axis, place, count in (("prow", prow_id, row_devs), ("pcol", pcol_id, col_devs)):
        for step in (1, count - 1):
            pl.semaphore_signal(
                barrier, 1, device_id={axis: lax.rem(place + step, count)}, device_id_type=mesh_ids
            )
    first[...] = moved_ref[:, :, :, 0:1, :]
    last[...] = moved_ref[:, :, :, chords - 1 : chords, :]
    pl.semaphore_wait(barrier, 4)

    def transfer(n, source, target, axis, place):
        return pltpu.make_async_remote_copy(
            src_ref=source,
            dst_ref=target,
            send_sem=send.at[n],
            recv_sem=recv.at[n],
            device_id={axis: place},
            device_id_type=mesh_ids,
        )

    upward = transfer(
        0, moved_ref.at[:, :, spans - 1], below, "prow", lax.rem(prow_id + 1, row_devs)
    )
    downward = transfer(
        1, moved_ref.at[:, :, 0], above, "prow", lax.rem(prow_id + row_devs - 1, row_devs)
    )
    onward = transfer(2, last, left, "pcol", lax.rem(pcol_id + 1, col_devs))
    backward = transfer(3, first, right, "pcol", lax.rem(pcol_id + col_devs - 1, col_devs))
    at_low, at_high = prow_id == 0, prow_id == row_devs - 1
    at_left, at_right = pcol_id == 0, pcol_id == col_devs - 1
    plans = (
        (upward, at_high, at_low),
        (downward, at_low, at_high),
        (onward, at_right, at_left),
        (backward, at_left, at_right),
    )
    for copy, closed, _ in plans:
        pl.when(jnp.logical_not(closed))(copy.start)

    @pl.when(at_low)
    def _():
        below[...] = 2.0 * moved_ref[:, :, 0] - moved_ref[:, :, 1]

    @pl.when(at_high)
    def _():
        above[...] = 2.0 * moved_ref[:, :, spans - 1] - moved_ref[:, :, spans - 2]

    @pl.when(at_left)
    def _():
        left[...] = 2.0 * moved_ref[:, :, :, 0:1, :] - moved_ref[:, :, :, 1:2, :]

    @pl.when(at_right)
    def _():
        right[...] = (
            2.0 * moved_ref[:, :, :, chords - 1 : chords, :]
            - moved_ref[:, :, :, chords - 2 : chords - 1, :]
        )

    for copy, closed, edge in plans:
        pl.when(jnp.logical_not(closed))(copy.wait_send)
        pl.when(jnp.logical_not(edge))(copy.wait_recv)

    chord_pos = lax.broadcasted_iota(jnp.int32, (3, chords, normals), 1)
    normal_pos = lax.broadcasted_iota(jnp.int32, (3, chords, normals), 2)

    @pl.loop(0, instances)
    def _(t):
        for s in range(spans):
            here = moved_ref[t, :, s]
            before = below[t] if s == 0 else moved_ref[t, :, s - 1]
            after = above[t] if s == spans - 1 else moved_ref[t, :, s + 1]
            d_span = (after - before) * scales[0]
            prior = jnp.where(chord_pos == 0, left[t, :, s], pltpu.roll(here, 1, 1))
            later = jnp.where(
                chord_pos == chords - 1, right[t, :, s], pltpu.roll(here, chords - 1, 1)
            )
            d_chord = (later - prior) * scales[1]
            up = pltpu.roll(here, normals - 1, 2)
            down = pltpu.roll(here, 1, 2)
            inner = jnp.where(normal_pos == 0, 2.0 * here - up, down)
            outer = jnp.where(normal_pos == normals - 1, 2.0 * here - down, up)
            d_normal = (outer - inner) * scales[2]
            out_ref[t, s] = (
                d_span[0] * (d_chord[1] * d_normal[2] - d_chord[2] * d_normal[1])
                + d_span[1] * (d_chord[2] * d_normal[0] - d_chord[0] * d_normal[2])
                + d_span[2] * (d_chord[0] * d_normal[1] - d_chord[1] * d_normal[0])
            )


def jacobian_of(moved):
    instances, _, spans, chords, normals = moved.shape
    row_devs, col_devs = lax.axis_size("prow"), lax.axis_size("pcol")
    scales = (spans * row_devs / 2.0, chords * col_devs / 2.0, normals / 2.0)
    vmem = pl.BlockSpec(memory_space=pltpu.VMEM)
    layer = pltpu.VMEM((instances, 3, chords, normals), jnp.float32)
    column = pltpu.VMEM((instances, 3, spans, 1, normals), jnp.float32)
    return pl.pallas_call(
        functools.partial(jacobian_kernel, scales, row_devs, col_devs),
        out_shape=jax.ShapeDtypeStruct((instances, spans, chords, normals), jnp.float32),
        in_specs=[vmem],
        out_specs=vmem,
        scratch_shapes=[
            column, column, layer, layer, column, column,
            pltpu.SemaphoreType.DMA((4,)), pltpu.SemaphoreType.DMA((4,)),
        ],
        compiler_params=pltpu.CompilerParams(
            collective_id=1, has_side_effects=True, vmem_limit_bytes=32 << 20
        ),
        name="jacobian",
    )(moved)


def halves(values):
    high = values.astype(jnp.bfloat16)
    return high, (values - high.astype(jnp.float32)).astype(jnp.bfloat16)


def product(values, high, low, dim):
    rows = values.shape[0]
    first, second = halves(values)
    dims = (((1,), (dim,)), ((), ()))
    both = lax.dot_general(
        jnp.concatenate([first, second], axis=0), high, dims, preferred_element_type=jnp.float32
    )
    rest = lax.dot_general(first, low, dims, preferred_element_type=jnp.float32)
    return both[:rows] + both[rows:] + rest


def solve_kernel(
    row_devs, col_devs, block_total, lower_ref, inverse_ref, right_ref, out_ref,
    lower_high, lower_low, inverse_high, inverse_low, forward, solved,
    parts, landed, joined, traded,
    part_send, part_recv, join_send, join_recv, trade_send, trade_recv, out_send, out_recv,
):
    prow_id = lax.axis_index("prow")
    pcol_id = lax.axis_index("pcol")
    pieces = parts.shape[1]
    base = (pcol_id // pieces) * pieces
    piece_id = lax.rem(pcol_id, pieces)
    mesh_ids = pl.DeviceIdType.MESH

    barrier = pltpu.get_barrier_semaphore()
    for o in range(1, col_devs):
        pl.semaphore_signal(
            barrier, 1, device_id={"pcol": lax.rem(pcol_id + o, col_devs)}, device_id_type=mesh_ids
        )
    for o in range(1, row_devs):
        pl.semaphore_signal(
            barrier, 1, device_id={"prow": lax.rem(prow_id + o, row_devs)}, device_id_type=mesh_ids
        )
    for p in range(lower_ref.shape[0]):
        lower_high[p], lower_low[p] = halves(lower_ref[p])
    for k in range(block_total):
        inverse_high[k], inverse_low[k] = halves(inverse_ref[k])
    pl.semaphore_wait(barrier, col_devs + row_devs - 2)

    def pair(i, j):
        return i * (i - 1) // 2 + j

    def sum_pcol(turn, values, meanwhile=None):
        for q in range(pieces):
            parts[turn, q] = values[:, q * 128 : (q + 1) * 128]
        copies = []
        for o in range(1, col_devs):
            other = lax.rem(pcol_id + o, col_devs)
            copy = pltpu.make_async_remote_copy(
                src_ref=parts.at[turn, lax.rem(other, pieces)],
                dst_ref=landed.at[turn, pcol_id],
                send_sem=part_send.at[o - 1],
                recv_sem=part_recv.at[turn, o - 1],
                device_id={"pcol": other},
                device_id_type=mesh_ids,
            )
            copy.start()
            copies.append(copy)
        landed[turn, pcol_id] = parts[turn, piece_id]
        extra = None if meanwhile is None else meanwhile()
        for copy in copies:
            copy.wait()
        total = landed[turn, 0]
        for d in range(1, col_devs):
            total = total + landed[turn, d]
        joined[turn, piece_id] = total
        copies = []
        for o in range(1, pieces):
            copy = pltpu.make_async_remote_copy(
                src_ref=joined.at[turn, piece_id],
                dst_ref=joined.at[turn, piece_id],
                send_sem=join_send.at[o - 1],
                recv_sem=join_recv.at[turn, o - 1],
                device_id={"pcol": base + lax.rem(piece_id + o, pieces)},
                device_id_type=mesh_ids,
            )
            copy.start()
            copies.append(copy)
        for copy in copies:
            copy.wait()
        return jnp.concatenate([joined[turn, q] for q in range(pieces)], axis=1), extra

    def sum_prow(turn, values, meanwhile=None):
        traded[turn, prow_id] = values
        copies = []
        for o in range(1, row_devs):
            copy = pltpu.make_async_remote_copy(
                src_ref=traded.at[turn, prow_id],
                dst_ref=traded.at[turn, prow_id],
                send_sem=trade_send.at[o - 1],
                recv_sem=trade_recv.at[turn, o - 1],
                device_id={"prow": lax.rem(prow_id + o, row_devs)},
                device_id_type=mesh_ids,
            )
            copy.start()
            copies.append(copy)
        extra = None if meanwhile is None else meanwhile()
        for copy in copies:
            copy.wait()
        total = traded[turn, 0]
        for d in range(1, row_devs):
            total = total + traded[turn, d]
        return total, extra

    def behind(k, known):
        partial = None
        for j in known:
            term = product(forward[j], lower_high[pair(k, j)], lower_low[pair(k, j)], 1)
            partial = term if partial is None else partial + term
        return partial

    def ahead(k, known):
        partial = None
        for j in known:
            term = product(solved[j, prow_id], lower_high[pair(j, k)], lower_low[pair(j, k)], 0)
            partial = term if partial is None else partial + term
        return partial

    def joint(early, late):
        return late if early is None else early + late

    col_turn = 0
    row_turn = 0
    for k in range(block_total):
        residual = right_ref[k]
        if k > 0:
            partial = joint(early, behind(k, [k - 1]))
            summed, _ = sum_pcol(col_turn, partial)
            residual = residual - summed
            col_turn += 1
        term = product(residual, inverse_high[k], inverse_low[k], 1)
        later = functools.partial(behind, k + 1, range(k)) if k + 1 < block_total else None
        forward[k], early = sum_prow(row_turn, term, later)
        row_turn += 1
    out_copies = []
    for k in reversed(range(block_total)):
        residual = forward[k]
        if k < block_total - 1:
            partial = joint(early, ahead(k, [k + 1]))
            summed, _ = sum_prow(row_turn, partial)
            residual = residual - summed
            row_turn += 1
        term = product(residual, inverse_high[k], inverse_low[k], 0)
        later = functools.partial(ahead, k - 1, range(k + 1, block_total)) if k > 0 else None
        solved[k, prow_id], early = sum_pcol(col_turn, term, later)
        col_turn += 1
        for o in range(1, row_devs):
            copy = pltpu.make_async_remote_copy(
                src_ref=solved.at[k, prow_id],
                dst_ref=solved.at[k, prow_id],
                send_sem=out_send.at[k, o - 1],
                recv_sem=out_recv.at[k, o - 1],
                device_id={"prow": lax.rem(prow_id + o, row_devs)},
                device_id_type=mesh_ids,
            )
            copy.start()
            out_copies.append(copy)
    for copy in out_copies:
        copy.wait()
    width = solved.shape[3]
    for k in range(block_total):
        for d in range(row_devs):
            start = (k * row_devs + d) * width
            out_ref[:, start : start + width] = solved[k, d]


def solve(local_factor, local_inverses, right_sides):
    row_devs = lax.axis_size("prow")
    col_devs = lax.axis_size("pcol")
    block_total, row_piece, _, col_piece = local_factor.shape
    row_count = right_sides.shape[0]
    lower = jnp.stack([local_factor[i, :, j] for i in range(block_total) for j in range(i)])
    own = right_sides.reshape(row_count, block_total, row_devs, row_piece)
    own = lax.dynamic_index_in_dim(own, lax.axis_index("prow"), 2, keepdims=False)
    own = own.transpose(1, 0, 2)
    pieces = row_piece // 128
    turns = 2 * block_total - 1
    vmem = pl.BlockSpec(memory_space=pltpu.VMEM)
    dma = pltpu.SemaphoreType.DMA
    narrow = jnp.bfloat16
    wide = jnp.float32
    return pl.pallas_call(
        functools.partial(solve_kernel, row_devs, col_devs, block_total),
        out_shape=jax.ShapeDtypeStruct((row_count, block_total * row_devs * row_piece), wide),
        in_specs=[vmem, vmem, vmem],
        out_specs=vmem,
        scratch_shapes=[
            pltpu.VMEM(lower.shape, narrow),
            pltpu.VMEM(lower.shape, narrow),
            pltpu.VMEM(local_inverses.shape, narrow),
            pltpu.VMEM(local_inverses.shape, narrow),
            pltpu.VMEM((block_total, row_count, col_piece), wide),
            pltpu.VMEM((block_total, row_devs, row_count, row_piece), wide),
            pltpu.VMEM((turns, pieces, row_count, 128), wide),
            pltpu.VMEM((turns, col_devs, row_count, 128), wide),
            pltpu.VMEM((turns, pieces, row_count, 128), wide),
            pltpu.VMEM((turns, row_devs, row_count, col_piece), wide),
            dma((col_devs - 1,)),
            dma((turns, col_devs - 1)),
            dma((pieces - 1,)),
            dma((turns, pieces - 1)),
            dma((row_devs - 1,)),
            dma((turns, row_devs - 1)),
            dma((block_total, row_devs - 1)),
            dma((block_total, row_devs - 1)),
        ],
        compiler_params=pltpu.CompilerParams(
            collective_id=0, has_side_effects=True, vmem_limit_bytes=40 << 20
        ),
        name="solve",
    )(lower, local_inverses, own)


def shards(factor, inverses, targets, anchors, nodes):
    row_devs = lax.axis_size("prow")
    local_factor = factor[:, 0, :, :, 0, :]
    local_inverses = inverses[:, 0, :, 0, :]
    block_total = local_factor.shape[0]
    row_piece = local_factor.shape[1]
    block_len = row_piece * row_devs
    instances = targets.shape[0]
    row_count = instances * targets.shape[1]
    point_total = targets.shape[2]
    right_sides = targets.reshape(row_count, block_total, block_len)
    coef_matrix = solve(local_factor, local_inverses, right_sides)
    shifts = deform(coef_matrix, anchors, nodes).reshape((instances,) + nodes.shape)
    moved = nodes[None] + 2.0 / math.sqrt(point_total) * shifts
    jacobian = jacobian_of(moved)
    return (coef_matrix.reshape(instances, 3, point_total), moved, jacobian)


def solution(mesh):
    placed = (
        P("blade", "prow", None, None, "pcol", None),
        P("blade", "pcol", None, "prow", None),
        P("blade", None, None),
        P("blade", None),
        P("blade", "prow", "pcol", None),
    )
    return jax.shard_map(
        shards,
        mesh=mesh,
        in_specs=placed,
        out_specs=(
            P("blade", None, None),
            P("blade", None, "prow", "pcol", None),
            P("blade", "prow", "pcol", None),
        ),
        check_vma=False,
    )
```
